32 devices in a mesh: dp: 4 (over y, core), ctx: 8 (over z, x).
Axes of the slice: x: 2, y: 2, z: 4, core: 2. Of those that a mesh axis runs over, the one named last changes fastest.
Arguments:
- inputs: bfloat16 [4096, 1536], P(('dp', 'ctx')), may hold values from -24 to 24
- positions: int32 [4096], P(('dp', 'ctx')), may hold values from 0 to 1023, as said below
- query_weight: bfloat16 [1536, 1536], P(('dp', 'ctx')), may hold values from -1 to 1
- key_projection: bfloat16 [1536, 768], P(('dp', 'ctx')), may hold values from -1 to 1
- value_projection: bfloat16 [1536, 768], P(('dp', 'ctx')), may hold values from -0.15625 to 0.15625
- out_weight: bfloat16 [1536, 1536], P(('dp', 'ctx')), may hold values from -1.25 to 1.25
- gate_weight: bfloat16 [1536, 4096], P(('dp', 'ctx')), may hold values from -0.15625 to 0.15625
- up_weight: bfloat16 [1536, 4096], P(('dp', 'ctx')), may hold values from -0.15625 to 0.15625
- down_weight: bfloat16 [4096, 1536], P(('dp', 'ctx')), may hold values from -0.09375 to 0.09375
- attn_gain: bfloat16 [1536], P(('dp', 'ctx')), may hold values from 0.5 to 1.5
- mlp_gain: bfloat16 [1536], P(('dp', 'ctx')), may hold values from 0.5 to 1.5
- cotangent: bfloat16 [4096, 1536], P(('dp', 'ctx')), may hold values from -6 to 6
Outputs:
- outputs: bfloat16 [4096, 1536], P(('dp', 'ctx'))
- grad_inputs: float32 [4096, 1536], P(('dp', 'ctx'))
- grad_query: float32 [1536, 1536], P(('dp', 'ctx'))
- grad_key: float32 [1536, 768], P(('dp', 'ctx'))
- grad_value: float32 [1536, 768], P(('dp', 'ctx'))
- grad_out: float32 [1536, 1536], P(('dp', 'ctx'))
- grad_gate: float32 [1536, 4096], P(('dp', 'ctx'))
- grad_up: float32 [1536, 4096], P(('dp', 'ctx'))
- grad_down: float32 [4096, 1536], P(('dp', 'ctx'))
- attn_gain_grad: float32 [1536], P(('dp', 'ctx'))
- mlp_gain_grad: float32 [1536], P(('dp', 'ctx'))
The draws below stay inside these ranges and needn't reach their ends.
Inputs may be any that keep to these rules, and one draw needn't show every extreme that they name: Each sequence holds every position once; each device's tokens are two runs of 64 rising consecutive positions, each starting at a multiple of 64.
All inputs are finite; a program needn't handle non-finite values.
Results may differ from the reference program's by a relative error of at most 0.035.
Values may be sent and summed in bfloat16 or wider, within the bound.
No kernel may reach another device: no remote copies, remote signals or barrier semaphores. Data moves between devices by JAX's collectives and lax.ppermute only.
A program may use at most 384 MiB of HBM per device.

```python
import math
import jax
import jax.numpy as jnp
from jax import lax

MODEL_WIDTH = 1536
QUERY_HEADS = 16
VALUE_HEADS = 8
HEAD_ENTRIES = 96
FEEDFWD_UNITS = 4096
TOK_DEV = 128
SEQUENCE_TOKENS = 1024
SEQS = 4
TOKENS = 4096
HALVES = 16
N_CTX = 8


def draw_inputs(key, part):
    row_key = jax.random.fold_in(key, 11)
    col_key = jax.random.fold_in(key, 12)
    base_key = jax.random.fold_in(key, 13)
    row_scale = jnp.exp(jax.random.uniform(row_key, (TOKENS, 1), jnp.float32, math.log(0.5), math.log(2.0)))
    col_scale = jnp.exp(jax.random.uniform(col_key, (1, MODEL_WIDTH), jnp.float32, math.log(0.3), math.log(3.0)))
    sampled_values = jax.random.normal(base_key, (TOKENS, MODEL_WIDTH), jnp.float32) * row_scale * col_scale
    return jnp.clip(sampled_values, -24.0, 24.0).astype(jnp.bfloat16)


def draw_query_weight(key, part):
    sampled_values = jax.random.normal(jax.random.fold_in(key, 21), (MODEL_WIDTH, QUERY_HEADS * HEAD_ENTRIES), jnp.float32) / math.sqrt(MODEL_WIDTH)
    return jnp.clip(sampled_values, -1.0, 1.0).astype(jnp.bfloat16)


def draw_key_projection(key, part):
    sampled_values = jax.random.normal(jax.random.fold_in(key, 22), (MODEL_WIDTH, VALUE_HEADS * HEAD_ENTRIES), jnp.float32) / math.sqrt(MODEL_WIDTH)
    return jnp.clip(sampled_values, -1.0, 1.0).astype(jnp.bfloat16)


def draw_positions(key, part):
    half_rows = TOK_DEV // 2

    def one_sequence(seq_index):
        order = jax.random.permutation(jax.random.fold_in(key, seq_index), HALVES)
        starts = order.astype(jnp.int32) * half_rows
        return (starts[:, None] + jnp.arange(half_rows, dtype=jnp.int32)[None, :]).reshape(SEQUENCE_TOKENS)
    return jax.vmap(one_sequence)(jnp.arange(SEQS, dtype=jnp.int32)).reshape(TOKENS).astype(jnp.int32)


def block_scale(own_key, dims, cuts, smallest, high):
    loudness, own = 1.0, jax.random.fold_in(own_key, 6)
    for position, shards_of in cuts:
        steps = jnp.exp(jax.random.uniform(jax.random.fold_in(own, position), (shards_of,), jnp.float32, smallest / len(cuts), high / len(cuts)))
        loudness = loudness * jnp.repeat(steps, dims[position] // shards_of).reshape([-1 if axis == position else 1 for axis in range(len(dims))])
    return loudness


def normal_values(rng, shape, deviation, limit, split=(), kind=jnp.bfloat16):
    level = block_scale(rng, shape, split, -0.22, 0.18) if split else 1.0
    drawn = jax.random.normal(rng, shape, jnp.float32) * deviation * level
    return jnp.minimum(jnp.maximum(drawn, -limit), limit).astype(kind)


def setup_inputs(seed: int = 0) -> dict:
    arg_keys = jax.random.split(jax.random.key(seed), 13)
    return {
        "inputs": draw_inputs(jax.random.fold_in(arg_keys[12], 71), 0),
        "positions": draw_positions(jax.random.fold_in(arg_keys[12], 71), 0),
        "query_weight": draw_query_weight(jax.random.fold_in(arg_keys[12], 71), 0),
        "key_projection": draw_key_projection(jax.random.fold_in(arg_keys[12], 71), 0),
        "value_projection": normal_values(arg_keys[4], (MODEL_WIDTH, VALUE_HEADS * HEAD_ENTRIES), MODEL_WIDTH ** -0.5, 0.15625, ((0, 32),)),
        "out_weight": normal_values(arg_keys[5], (QUERY_HEADS * HEAD_ENTRIES, MODEL_WIDTH), (max(4, QUERY_HEADS * HEAD_ENTRIES * 16 // (TOK_DEV * N_CTX))) ** -0.5, 1.25, ((0, 32),)),
        "gate_weight": normal_values(arg_keys[6], (MODEL_WIDTH, FEEDFWD_UNITS), MODEL_WIDTH ** -0.5, 0.15625, ((0, 32),)),
        "up_weight": normal_values(arg_keys[7], (MODEL_WIDTH, FEEDFWD_UNITS), MODEL_WIDTH ** -0.5, 0.15625, ((0, 32),)),
        "down_weight": normal_values(arg_keys[8], (FEEDFWD_UNITS, MODEL_WIDTH), FEEDFWD_UNITS ** -0.5, 0.09375, ((0, 32),)),
        "attn_gain": jnp.clip(1.0 + 0.1 * jax.random.normal(arg_keys[9], (MODEL_WIDTH,), jnp.float32), 0.5, 1.5).astype(jnp.bfloat16),
        "mlp_gain": jnp.clip(1.0 + 0.1 * jax.random.normal(arg_keys[10], (MODEL_WIDTH,), jnp.float32), 0.5, 1.5).astype(jnp.bfloat16),
        "cotangent": normal_values(arg_keys[11], (TOKENS, MODEL_WIDTH), 1.0, 6.0, ((0, 32),)),
    }


NORM_EPS = 1e-05
ROPE_BASE = 100000.0
BLOCKED_SCORE = -1e+30

def rope_tables(token_pos):
    half_width = HEAD_ENTRIES // 2
    inverse = ROPE_BASE ** (-2.0 * jnp.arange(half_width, dtype=jnp.float32) / HEAD_ENTRIES)
    angles = token_pos.astype(jnp.float32)[:, None] * inverse[None, :]
    return (jnp.cos(angles), jnp.sin(angles))

def apply_rotation(vectors, cosine_lookup, sine_lookup, rot_sign):
    half_width = vectors.shape[-1] // 2
    lower_half = vectors[..., :half_width]
    upper_half = vectors[..., half_width:]
    cosine_part = cosine_lookup[:, None, :]
    sine_part = rot_sign * sine_lookup[:, None, :]
    return jnp.concatenate([lower_half * cosine_part - upper_half * sine_part, upper_half * cosine_part + lower_half * sine_part], axis=-1)

def rounded(values):
    return lax.optimization_barrier(values.astype(jnp.bfloat16)).astype(jnp.float32)

def reference(inputs, positions, query_weight, key_projection, value_projection, out_weight, gate_weight, up_weight, down_weight, attn_gain, mlp_gain, cotangent):
    heads_per_group = QUERY_HEADS // VALUE_HEADS
    score_scale = 1.0 / math.sqrt(HEAD_ENTRIES)
    rows_per_block = min(512, SEQUENCE_TOKENS)
    count_of_blocks = SEQUENCE_TOKENS // rows_per_block
    gain_one = attn_gain.astype(jnp.float32)
    gain_two = mlp_gain.astype(jnp.float32)

    def sequence_step(grad_carry, seq_item):
        seq_inputs, seq_pos, seq_cot = seq_item
        input_f32 = seq_inputs.astype(jnp.float32)
        inv_rms1 = lax.rsqrt(lax.optimization_barrier(jnp.mean(input_f32 * input_f32, axis=1, keepdims=True)) + NORM_EPS)
        normalized_attention = (input_f32 * inv_rms1 * gain_one).astype(jnp.bfloat16)
        cosine_lookup, sine_lookup = rope_tables(seq_pos)
        query_vectors = apply_rotation(jnp.dot(normalized_attention, query_weight, preferred_element_type=jnp.float32).reshape(SEQUENCE_TOKENS, QUERY_HEADS, HEAD_ENTRIES), cosine_lookup, sine_lookup, 1.0).astype(jnp.bfloat16)
        key_matrix_rows = apply_rotation(jnp.dot(normalized_attention, key_projection, preferred_element_type=jnp.float32).reshape(SEQUENCE_TOKENS, VALUE_HEADS, HEAD_ENTRIES), cosine_lookup, sine_lookup, 1.0).astype(jnp.bfloat16)
        value_matrix_rows = jnp.dot(normalized_attention, value_projection, preferred_element_type=jnp.float32).astype(jnp.bfloat16).reshape(SEQUENCE_TOKENS, VALUE_HEADS, HEAD_ENTRIES)
        blocked_queries = query_vectors.reshape(count_of_blocks, rows_per_block, VALUE_HEADS, heads_per_group, HEAD_ENTRIES)
        pos_blocks = seq_pos.reshape(count_of_blocks, rows_per_block)
        key_f32 = key_matrix_rows.astype(jnp.float32)
        value_f32 = value_matrix_rows.astype(jnp.float32)

        def forward_block(unused, block_item):
            query_block, query_pos = block_item
            visible = seq_pos[None, :] <= query_pos[:, None]
            scores = jnp.einsum('qgjd,kgd->gjqk', query_block.astype(jnp.float32), key_f32) * score_scale
            scores = jnp.where(visible, scores, BLOCKED_SCORE)
            row_top = lax.optimization_barrier(jnp.max(scores, axis=-1))
            probs = jnp.where(visible, jnp.exp(scores - row_top[..., None]), 0.0)
            row_total = lax.optimization_barrier(jnp.sum(probs, axis=-1))
            weighted = jnp.einsum('gjqk,kgd->gjqd', rounded(probs), value_f32)
            attn_block = jnp.transpose(weighted / row_total[..., None], (2, 0, 1, 3)).astype(jnp.bfloat16)
            return (unused, (attn_block, row_top + jnp.log(row_total)))
        unused_end, (attn_blocks, log_totals) = lax.scan(forward_block, jnp.zeros((), jnp.float32), (blocked_queries, pos_blocks))
        attention_rows = attn_blocks.reshape(SEQUENCE_TOKENS, QUERY_HEADS * HEAD_ENTRIES)
        residual = input_f32 + jnp.dot(attention_rows, out_weight, preferred_element_type=jnp.float32)
        inv_rms2 = lax.rsqrt(lax.optimization_barrier(jnp.mean(residual * residual, axis=1, keepdims=True)) + NORM_EPS)
        normed_mlp = (residual * inv_rms2 * gain_two).astype(jnp.bfloat16)
        gate_proj = jnp.dot(normed_mlp, gate_weight, preferred_element_type=jnp.float32)
        up_proj = jnp.dot(normed_mlp, up_weight, preferred_element_type=jnp.float32)
        gate_sigmoid = jax.nn.sigmoid(gate_proj)
        hidden_act = (gate_proj * gate_sigmoid * up_proj).astype(jnp.bfloat16)
        outputs = (residual + jnp.dot(hidden_act, down_weight, preferred_element_type=jnp.float32)).astype(jnp.bfloat16)
        d_act = jnp.dot(seq_cot, down_weight.T, preferred_element_type=jnp.float32)
        grad_down = jnp.dot(hidden_act.T, seq_cot, preferred_element_type=jnp.float32)
        d_gate = (d_act * up_proj * gate_sigmoid * (1.0 + gate_proj * (1.0 - gate_sigmoid))).astype(jnp.bfloat16)
        d_up = (d_act * gate_proj * gate_sigmoid).astype(jnp.bfloat16)
        grad_gate = jnp.dot(normed_mlp.T, d_gate, preferred_element_type=jnp.float32)
        grad_up = jnp.dot(normed_mlp.T, d_up, preferred_element_type=jnp.float32)
        d_normed_mlp = jnp.dot(d_gate, gate_weight.T, preferred_element_type=jnp.float32) + jnp.dot(d_up, up_weight.T, preferred_element_type=jnp.float32)
        grad_gain_two = lax.optimization_barrier(jnp.sum(d_normed_mlp * residual * inv_rms2, axis=0))
        scaled_two = d_normed_mlp * gain_two
        d_residual = seq_cot.astype(jnp.float32) + inv_rms2 * scaled_two - residual * inv_rms2 ** 3 * lax.optimization_barrier(jnp.mean(scaled_two * residual, axis=1, keepdims=True))
        d_res_round = d_residual.astype(jnp.bfloat16)
        grad_out = jnp.dot(attention_rows.T, d_res_round, preferred_element_type=jnp.float32)
        attention_gradient = jnp.dot(d_res_round, out_weight.T, preferred_element_type=jnp.float32).astype(jnp.bfloat16)
        row_difference = lax.optimization_barrier(jnp.sum(attention_gradient.astype(jnp.float32).reshape(SEQUENCE_TOKENS, VALUE_HEADS, heads_per_group, HEAD_ENTRIES) * attention_rows.astype(jnp.float32).reshape(SEQUENCE_TOKENS, VALUE_HEADS, heads_per_group, HEAD_ENTRIES), axis=-1))
        difference_blocks = jnp.transpose(row_difference.reshape(count_of_blocks, rows_per_block, VALUE_HEADS, heads_per_group), (0, 2, 3, 1))
        attention_gradient_blocks = attention_gradient.reshape(count_of_blocks, rows_per_block, VALUE_HEADS, heads_per_group, HEAD_ENTRIES)

        def backward_block(pair_carry, block_item):
            key_gradient, value_gradient = pair_carry
            query_block, query_pos, d_block, log_total, delta_block = block_item
            visible = seq_pos[None, :] <= query_pos[:, None]
            scores = jnp.einsum('qgjd,kgd->gjqk', query_block.astype(jnp.float32), key_f32) * score_scale
            probs_back = jnp.where(visible, jnp.exp(jnp.where(visible, scores, BLOCKED_SCORE) - log_total[..., None]), 0.0)
            d_block_f32 = d_block.astype(jnp.float32)
            value_gradient = value_gradient + jnp.einsum('gjqk,qgjd->kgd', rounded(probs_back), d_block_f32)
            d_probs = jnp.einsum('qgjd,kgd->gjqk', d_block_f32, value_f32)
            d_scores = rounded(score_scale * probs_back * (d_probs - delta_block[..., None]))
            d_queries = jnp.einsum('gjqk,kgd->qgjd', d_scores, key_f32)
            key_gradient = key_gradient + jnp.einsum('gjqk,qgjd->kgd', d_scores, query_block.astype(jnp.float32))
            return ((key_gradient, value_gradient), d_queries)
        empty_rows = jnp.zeros((SEQUENCE_TOKENS, VALUE_HEADS, HEAD_ENTRIES), jnp.float32)
        (key_gradient, value_gradient), d_queries = lax.scan(backward_block, (empty_rows, empty_rows), (blocked_queries, pos_blocks, attention_gradient_blocks, log_totals, difference_blocks))
        dq_rot = apply_rotation(d_queries.reshape(SEQUENCE_TOKENS, QUERY_HEADS, HEAD_ENTRIES), cosine_lookup, sine_lookup, -1.0).astype(jnp.bfloat16).reshape(SEQUENCE_TOKENS, QUERY_HEADS * HEAD_ENTRIES)
        key_gradient_rotated = apply_rotation(key_gradient, cosine_lookup, sine_lookup, -1.0).astype(jnp.bfloat16).reshape(SEQUENCE_TOKENS, VALUE_HEADS * HEAD_ENTRIES)
        value_gradient_rounded = value_gradient.astype(jnp.bfloat16).reshape(SEQUENCE_TOKENS, VALUE_HEADS * HEAD_ENTRIES)
        grad_query = jnp.dot(normalized_attention.T, dq_rot, preferred_element_type=jnp.float32)
        grad_key = jnp.dot(normalized_attention.T, key_gradient_rotated, preferred_element_type=jnp.float32)
        grad_value = jnp.dot(normalized_attention.T, value_gradient_rounded, preferred_element_type=jnp.float32)
        d_normed_attn = jnp.dot(dq_rot, query_weight.T, preferred_element_type=jnp.float32) + jnp.dot(key_gradient_rotated, key_projection.T, preferred_element_type=jnp.float32) + jnp.dot(value_gradient_rounded, value_projection.T, preferred_element_type=jnp.float32)
        grad_gain_one = lax.optimization_barrier(jnp.sum(d_normed_attn * input_f32 * inv_rms1, axis=0))
        scaled_one = d_normed_attn * gain_one
        grad_inputs = d_residual + inv_rms1 * scaled_one - input_f32 * inv_rms1 ** 3 * lax.optimization_barrier(jnp.mean(scaled_one * input_f32, axis=1, keepdims=True))
        fresh = (grad_query, grad_key, grad_value, grad_out, grad_gate, grad_up, grad_down, grad_gain_one, grad_gain_two)
        summed = tuple((older + newer for older, newer in zip(grad_carry, fresh)))
        return (summed, (outputs, grad_inputs))
    initial_gradients = (jnp.zeros((MODEL_WIDTH, QUERY_HEADS * HEAD_ENTRIES), jnp.float32), jnp.zeros((MODEL_WIDTH, VALUE_HEADS * HEAD_ENTRIES), jnp.float32), jnp.zeros((MODEL_WIDTH, VALUE_HEADS * HEAD_ENTRIES), jnp.float32), jnp.zeros((QUERY_HEADS * HEAD_ENTRIES, MODEL_WIDTH), jnp.float32), jnp.zeros((MODEL_WIDTH, FEEDFWD_UNITS), jnp.float32), jnp.zeros((MODEL_WIDTH, FEEDFWD_UNITS), jnp.float32), jnp.zeros((FEEDFWD_UNITS, MODEL_WIDTH), jnp.float32), jnp.zeros((MODEL_WIDTH,), jnp.float32), jnp.zeros((MODEL_WIDTH,), jnp.float32))
    grads, (seq_outputs, seq_grads) = lax.scan(sequence_step, initial_gradients, (inputs.reshape(SEQS, SEQUENCE_TOKENS, MODEL_WIDTH), positions.reshape(SEQS, SEQUENCE_TOKENS), cotangent.reshape(SEQS, SEQUENCE_TOKENS, MODEL_WIDTH)))
    return (seq_outputs.reshape(TOKENS, MODEL_WIDTH), seq_grads.reshape(TOKENS, MODEL_WIDTH), grads[0], grads[1], grads[2], grads[3], grads[4], grads[5], grads[6], grads[7], grads[8])
```

```python
import math

import jax
import jax.numpy as jnp
from jax import lax
from jax.sharding import Mesh
from jax.sharding import PartitionSpec as P

QUERY_HEADS = 16
VALUE_HEADS = 8
HEAD_ENTRIES = 96
GROUP = QUERY_HEADS // VALUE_HEADS

NORM_EPS = 1e-05
ROPE_BASE = 100000.0
BLOCKED_SCORE = -1e30

BF = jnp.bfloat16
F32 = jnp.float32

ALL = ("y", "core", "r", "s", "b")
PLANE = ("y", "core", "b")
LINE = ("r", "s")
OFFSETS = tuple((y, c, b) for c in (0, 1) for y in (0, 1) for b in (0, 1))


def dot(a, b):
    return jnp.dot(a, b, preferred_element_type=F32)


def dot_tn(a, b):
    return lax.dot_general(a, b, (((0,), (0,)), ((), ())), preferred_element_type=F32)


def dot_nt(a, b):
    return lax.dot_general(a, b, (((1,), (1,)), ((), ())), preferred_element_type=F32)


def flip(value, axis):
    return lax.ppermute(value, axis, [(0, 1), (1, 0)])


def plane_pairs(first, second):
    pairs = []
    for y in (0, 1):
        for c in (0, 1):
            for b in (0, 1):
                way = first if c == 0 else second
                to = (1 - y, c, b) if way == "y" else (y, c, 1 - b)
                pairs.append(((y * 2 + c) * 2 + b, (to[0] * 2 + to[1]) * 2 + to[2]))
    return pairs


def plane_gather(own):
    core = lax.axis_index("core")
    by_b = flip(own, "b")
    by_y = flip(own, "y")
    diag = lax.ppermute(jnp.where(core == 0, by_b, by_y), PLANE, plane_pairs("y", "b"))
    return [own, by_b, by_y, diag] + [flip(v, "core") for v in (own, by_b, by_y, diag)]


def plane_scatter(parts):
    core = lax.axis_index("core")
    theirs = flip(parts[4:], "core")
    own, by_b, by_y, diag = [parts[k].astype(F32) + theirs[k].astype(F32) for k in range(4)]
    sent = jnp.stack([jnp.where(core == 0, by_b, by_y).astype(BF), diag.astype(BF)])
    got = lax.ppermute(sent, PLANE, plane_pairs("b", "y")).astype(F32)
    last = (jnp.where(core == 0, by_y, by_b) + got[1]).astype(BF)
    return own + got[0] + lax.ppermute(last, PLANE, plane_pairs("y", "b")).astype(F32)


def rope_tables(token_pos):
    half_width = HEAD_ENTRIES // 2
    inverse = ROPE_BASE ** (-2.0 * jnp.arange(half_width, dtype=F32) / HEAD_ENTRIES)
    angles = token_pos.astype(F32)[:, None] * inverse[None, :]
    return (jnp.cos(angles), jnp.sin(angles))


def apply_rotation(vectors, cosine, sine, rot_sign):
    half_width = vectors.shape[-1] // 2
    low, high = vectors[..., :half_width], vectors[..., half_width:]
    sine = rot_sign * sine
    return jnp.concatenate([low * cosine - high * sine, high * cosine + low * sine], axis=-1)


def body(sizes, inputs, positions, wq, wk, wv, wo, wg, wu, wd, attn_gain, mlp_gain, cotangent):
    D, R, S, B = sizes
    RS, T = R * S, D * B
    HE = HEAD_ENTRIES
    rows = inputs.shape[0]
    width = inputs.shape[1]
    I = wq.shape[0]
    FF = wg.shape[1]
    J = FF // (D * RS * B)
    y, core, r, s, b = [lax.axis_index(a) for a in ALL]
    dp = y * 2 + core
    scale = 1.0 / math.sqrt(HE)
    gain1 = attn_gain.astype(F32)[:, None]
    gain2 = mlp_gain.astype(F32)[:, None]

    def natural(w):
        cols = w.shape[-1]
        return w.reshape(RS, D, B * I, cols).transpose(1, 0, 2, 3).reshape(width, cols)

    def by_line(g):
        cols = g.shape[-1]
        return g.reshape(D, RS, B * I, cols).transpose(1, 0, 2, 3).reshape(width, cols)

    def to_columns(blocks):
        got = lax.all_to_all(blocks, PLANE, split_axis=0, concat_axis=0, tiled=True)
        full = lax.all_gather(got.reshape(T * I, -1), LINE, axis=0, tiled=True)
        return natural(full)

    def to_rows(grad):
        mine = lax.psum_scatter(by_line(grad).astype(BF), LINE, scatter_dimension=0, tiled=True)
        return lax.all_to_all(
            mine.reshape(T, I, -1), PLANE, split_axis=0, concat_axis=0, tiled=True
        )

    def heads_of(w, n):
        return w.reshape(I, T, n).transpose(1, 0, 2)

    def units_of(w):
        return w.reshape(I, D, RS, B, J).transpose(1, 3, 0, 2, 4).reshape(T, I, RS * J)

    def scaled(w, gain):
        return (w.astype(F32) * gain).astype(BF)

    swap = []
    for i0 in range(D):
        for ir in range(R):
            for i1 in range(S):
                for ib in range(B):
                    swap.append(
                        (((i0 * R + ir) * S + i1) * B + ib, ((i1 * R + ir) * S + i0) * B + ib)
                    )
    x_bf = lax.ppermute(inputs, ALL, swap)
    cot_bf = lax.ppermute(cotangent, ALL, swap)
    pos_all = lax.all_gather(positions, ALL, axis=0, tiled=True).reshape(D, R, T, rows)
    seats = jnp.stack([((y ^ oy) * 2 + (core ^ oc)) * B + (b ^ ob) for oy, oc, ob in OFFSETS])
    pos_seq = lax.dynamic_index_in_dim(pos_all, s, 0, keepdims=False)
    pos_seq = jnp.take(pos_seq, seats, axis=1)
    key_pos = pos_seq.reshape(-1)
    pos = lax.dynamic_index_in_dim(pos_seq, r, 0, keepdims=False).reshape(-1)
    tokens = pos.shape[0]

    qkv_blocks = jnp.concatenate(
        [heads_of(scaled(wq, gain1), GROUP * HE), heads_of(scaled(wk, gain1), HE)]
        + [heads_of(scaled(wv, gain1), HE)],
        axis=-1,
    )
    w_qkv = to_columns(qkv_blocks)
    half = RS // 2
    wo_line = lax.all_gather(wo, LINE, axis=0, tiled=True).reshape(RS, I, width)
    kept = lax.dynamic_slice_in_dim(wo_line, b * half, half)
    got = flip(lax.dynamic_slice_in_dim(wo_line, (1 - b) * half, half), "b")
    w_o = jnp.where(b == 0, jnp.stack([kept, got], 1), jnp.stack([got, kept], 1))
    w_o = w_o.reshape(GROUP * HE, width)
    w_gu = to_columns(
        jnp.concatenate([units_of(scaled(wg, gain2)), units_of(scaled(wu, gain2))], axis=-1)
    )
    w_d = lax.all_gather(wd, LINE, axis=0, tiled=True)

    x = x_bf.astype(F32)
    inv1 = lax.rsqrt(jnp.mean(x * x, axis=1, keepdims=True) + NORM_EPS)
    xh = jnp.concatenate(plane_gather((x * inv1).astype(BF)), axis=0)
    cos, sin = rope_tables(pos)
    qkv = dot(xh, w_qkv)
    q = apply_rotation(
        qkv[:, : GROUP * HE].reshape(tokens, GROUP, HE), cos[:, None], sin[:, None], 1.0
    ).astype(BF)
    k = apply_rotation(qkv[:, GROUP * HE : (GROUP + 1) * HE], cos, sin, 1.0).astype(BF)
    v = qkv[:, (GROUP + 1) * HE :].astype(BF)
    if R > 1:
        k = lax.all_gather(k, "r", axis=0, tiled=True)
        v = lax.all_gather(v, "r", axis=0, tiled=True)
    visible = key_pos[None, :] <= pos[:, None]
    scores = jnp.einsum("qjd,kd->jqk", q, k, preferred_element_type=F32) * scale
    scores = jnp.where(visible, scores, BLOCKED_SCORE)
    top = jnp.max(scores, axis=-1, keepdims=True)
    probs = jnp.where(visible, jnp.exp(scores - top), 0.0)
    total = jnp.sum(probs, axis=-1, keepdims=True)
    o = jnp.einsum("jqk,kd->jqd", probs.astype(BF), v, preferred_element_type=F32) / total
    log_total = top + jnp.log(total)
    o = jnp.transpose(o, (1, 0, 2)).astype(BF).reshape(tokens, GROUP * HE)
    residual = x + plane_scatter(dot(o, w_o).astype(BF).reshape(T, rows, width))

    cot_all = jnp.concatenate(plane_gather(cot_bf), axis=0)
    inv2 = lax.rsqrt(jnp.mean(residual * residual, axis=1, keepdims=True) + NORM_EPS)
    mh = jnp.concatenate(plane_gather((residual * inv2).astype(BF)), axis=0)
    gu = dot(mh, w_gu)
    gate, up = gu[:, : RS * J], gu[:, RS * J :]
    sig = jax.nn.sigmoid(gate)
    hidden = (gate * sig * up).astype(BF)
    d_act = dot_nt(cot_all, w_d)
    d_gate = d_act * up * sig * (1.0 + gate * (1.0 - sig))
    d_up = d_act * gate * sig
    d_gu = jnp.concatenate([d_gate.astype(BF), d_up.astype(BF)], axis=1)
    u2 = plane_scatter(dot_nt(d_gu, w_gu).astype(BF).reshape(T, rows, width))
    out_own = residual + plane_scatter(dot(hidden, w_d).astype(BF).reshape(T, rows, width))
    outputs = lax.ppermute(out_own.astype(BF), ALL, swap)
    grad_down = lax.psum_scatter(
        dot_tn(hidden, cot_all).astype(BF), LINE, scatter_dimension=0, tiled=True
    ).astype(F32)
    rows_gu = to_rows(dot_tn(mh, d_gu)).astype(F32).reshape(D, B, I, 2, RS, J)
    rows_gu = rows_gu.transpose(3, 2, 0, 4, 1, 5).reshape(2, I, FF)
    mlp_gain_grad = jnp.sum(
        rows_gu[0] * wg.astype(F32) + rows_gu[1] * wu.astype(F32), axis=1
    )
    grad_gate, grad_up = rows_gu[0] * gain2, rows_gu[1] * gain2
    d_res = (
        cot_bf.astype(F32)
        + inv2 * u2
        - residual * inv2**3 * jnp.mean(u2 * residual, axis=1, keepdims=True)
    )

    dr = jnp.concatenate(plane_gather(d_res.astype(BF)), axis=0)
    g_o = dot_tn(o, dr).astype(BF).reshape(half, B, I, width)
    g_keep = lax.dynamic_index_in_dim(g_o, b, 1, keepdims=False)
    g_got = flip(lax.dynamic_index_in_dim(g_o, 1 - b, 1, keepdims=False), "b")
    g_line = jnp.where(
        b == 0, jnp.concatenate([g_keep, g_got]), jnp.concatenate([g_got, g_keep])
    ).reshape(RS * I, width)
    grad_out = lax.psum_scatter(g_line, LINE, scatter_dimension=0, tiled=True).astype(F32)
    d_o = dot_nt(dr, w_o).astype(BF)
    d_o3, o3 = d_o.reshape(tokens, GROUP, HE), o.reshape(tokens, GROUP, HE)
    delta = jnp.sum(d_o3.astype(F32) * o3.astype(F32), axis=-1).T[..., None]
    probs_back = jnp.where(visible, jnp.exp(scores - log_total), 0.0)
    dv = jnp.einsum("jqk,qjd->kd", probs_back.astype(BF), d_o3, preferred_element_type=F32)
    d_probs = jnp.einsum("qjd,kd->jqk", d_o3, v, preferred_element_type=F32)
    d_scores = (scale * probs_back * (d_probs - delta)).astype(BF)
    dq = jnp.einsum("jqk,kd->qjd", d_scores, k, preferred_element_type=F32)
    dk = jnp.einsum("jqk,qjd->kd", d_scores, q, preferred_element_type=F32)
    if R > 1:
        dk = lax.psum_scatter(dk.astype(BF), "r", scatter_dimension=0, tiled=True).astype(F32)
        dv = lax.psum_scatter(dv.astype(BF), "r", scatter_dimension=0, tiled=True)
    dq_rot = apply_rotation(dq, cos[:, None], sin[:, None], -1.0).reshape(tokens, GROUP * HE)
    dk_rot = apply_rotation(dk, cos, sin, -1.0)
    d_qkv = jnp.concatenate([dq_rot.astype(BF), dk_rot.astype(BF), dv.astype(BF)], axis=1)
    u1 = plane_scatter(dot_nt(d_qkv, w_qkv).astype(BF).reshape(T, rows, width))
    rows_qkv = to_rows(dot_tn(xh, d_qkv)).astype(F32)
    rows_q = rows_qkv[:, :, : GROUP * HE].transpose(1, 0, 2).reshape(I, -1)
    rows_k = rows_qkv[:, :, GROUP * HE : (GROUP + 1) * HE].transpose(1, 0, 2).reshape(I, -1)
    rows_v = rows_qkv[:, :, (GROUP + 1) * HE :].transpose(1, 0, 2).reshape(I, -1)
    attn_gain_grad = (
        jnp.sum(rows_q * wq.astype(F32), axis=1)
        + jnp.sum(rows_k * wk.astype(F32), axis=1)
        + jnp.sum(rows_v * wv.astype(F32), axis=1)
    )
    gx_own = (
        d_res + inv1 * u1 - x * inv1**3 * jnp.mean(u1 * x, axis=1, keepdims=True)
    )
    grad_inputs = lax.ppermute(gx_own.astype(BF), ALL, swap).astype(F32)
    return (
        outputs,
        grad_inputs,
        rows_q * gain1,
        rows_k * gain1,
        rows_v * gain1,
        grad_out,
        grad_gate,
        grad_up,
        grad_down,
        attn_gain_grad,
        mlp_gain_grad,
    )


def solution(mesh):
    D, C = mesh.shape["dp"], mesh.shape["ctx"]
    B = VALUE_HEADS // D
    S = D
    R = C // (S * B)
    assert D == 4 and B == 2 and R * S * B == C
    fine = Mesh(mesh.devices.reshape(2, 2, R, S, B), ALL)
    wide, flat = P(ALL, None), P(ALL)

    def step(*args):
        return body((D, R, S, B), *args)

    return jax.shard_map(
        step,
        mesh=fine,
        in_specs=(wide, flat, wide, wide, wide, wide, wide, wide, wide, flat, flat, wide),
        out_specs=(wide,) * 9 + (flat, flat),
        check_vma=False,
    )
```
